32 devices in a mesh: seq: 16 (over z, y, x), grp: 2 (over core).
Axes of the slice: x: 2, y: 2, z: 4, core: 2. Of those that a mesh axis runs over, the one named last changes fastest.
Arguments:
- key_rows: bfloat16 [32768, 4096], P('seq', 'grp')
- probe_ints: int32 [4096, 512], P('grp'), may hold values from -2 to 2
- rank_keep: int32 [1], replicated, may hold values from 128 to 511
Outputs:
- latents: float32 [32768, 512], P('seq', 'grp')
- latent_basis: float32 [512, 4096], P('seq', 'grp')
The draws below stay inside these ranges and needn't reach their ends.
All inputs are finite; a program needn't handle non-finite values.
Results may differ from the reference program's by a relative error of at most 0.00098.
Values may be sent and summed in bfloat16 or wider, within the bound.
A program may use at most 128 MiB of HBM per device.

```python
import math
import jax
import jax.numpy as jnp
from jax import lax

W = 4096
P_SIZE = 512
TOKENS = 32768


def draw_key_rows(key, part):
    first, second, third = jax.random.split(jax.random.fold_in(key, 17), 3)
    values = jax.random.normal(first, (TOKENS, W), jnp.float32)
    row_scale = jnp.exp(jax.random.uniform(second, (TOKENS, 1), jnp.float32) * math.log(10.0))
    col_scale = jnp.exp(jax.random.uniform(third, (1, W), jnp.float32, math.log(0.3), math.log(3.0)))
    result = values * row_scale * col_scale
    return result.astype(jnp.bfloat16)


def with_ends(entries, rng, least, top_value):
    dims = entries.shape
    spot = [jax.random.randint(jax.random.fold_in(rng, axis), (), 0, dims[axis]) for axis in range(len(dims))]
    entries = entries.at[tuple(spot)].set(least)
    longest = dims.index(max(dims))
    spot[longest] = (spot[longest] + 1) % dims[longest]
    return entries.at[tuple(spot)].set(top_value)


def setup_inputs(seed: int = 0) -> dict:
    key_of = jax.random.split(jax.random.key(seed), 4)
    key_rows = draw_key_rows(jax.random.fold_in(key_of[3], 71), 0)
    probe_ints = with_ends(jax.random.randint(key_of[1], (W, P_SIZE), -2, 3), jax.random.fold_in(key_of[1], 1), -2, 2).astype(jnp.int32)
    rank_keep = jax.random.randint(key_of[2], (1,), P_SIZE // 4, P_SIZE).astype(jnp.int32)
    return {"key_rows": key_rows, "probe_ints": probe_ints, "rank_keep": rank_keep}


def reference(key_rows, probe_ints, rank_keep):
    tokens = key_rows.shape[0]
    root_tokens = math.sqrt(tokens)
    probes = (probe_ints.astype(jnp.float32) * 0.015625).astype(jnp.bfloat16)
    sketch = jnp.dot(key_rows.astype(jnp.float32), probes.astype(jnp.float32), preferred_element_type=jnp.float32)
    gram_matrix = lax.dot_general(sketch, sketch, (((0,), (0,)), ((), ())), precision=lax.Precision.HIGHEST)
    lower_factor = jnp.linalg.cholesky(gram_matrix)
    identity = jnp.eye(gram_matrix.shape[0], dtype=jnp.float32)
    inverse = lax.linalg.triangular_solve(lower_factor, identity, left_side=True, lower=True)
    orthonormal = jnp.dot(sketch, inverse.T, precision=lax.Precision.HIGHEST) * root_tokens
    columns = jnp.arange(orthonormal.shape[1]).astype(jnp.int32)
    keep_mask = columns < rank_keep[0]
    latents = jnp.where(keep_mask[None, :], orthonormal, jnp.float32(0.0))
    rounded = orthonormal.astype(jnp.bfloat16)
    product = lax.dot_general(rounded.astype(jnp.float32), key_rows.astype(jnp.float32), (((0,), (0,)), ((), ())), preferred_element_type=jnp.float32)
    latent_basis = jnp.where(keep_mask[:, None], product / root_tokens, jnp.float32(0.0))
    return (latents, latent_basis)
```

```python
import functools
import math

import jax
import jax.numpy as jnp
from jax import lax
from jax.experimental import pallas as pl
from jax.experimental.pallas import tpu as pltpu
from jax.sharding import PartitionSpec as P

MESH = pl.DeviceIdType.MESH
BLOCK = 128
LAST = (((1,), (1,)), ((), ()))


def dot_f32(a, b, dims=(((1,), (0,)), ((), ()))):
    return lax.dot_general(a, b, dims, preferred_element_type=jnp.float32)


def front_kernel(
    chunk, tile, keys_hbm, ints_hbm, sketch_ref, gram_ref, basis_ref,
    keys, ints, probes, part, other, high, low, key_sem, int_sem, send_sem, recv_sem,
):
    tokens, width = keys.shape
    group = lax.axis_index("grp")
    peer = 1 - group
    chunks = tokens // chunk

    def key_copy(i):
        rows = pl.ds(pl.multiple_of(i * chunk, chunk), chunk)
        return pltpu.make_async_copy(keys_hbm.at[rows], keys.at[rows], key_sem.at[i])

    def swap(i):
        rows = pl.ds(pl.multiple_of(i * chunk, chunk), chunk)
        return pltpu.make_async_remote_copy(
            src_ref=part.at[rows], dst_ref=other.at[rows],
            send_sem=send_sem.at[i], recv_sem=recv_sem.at[i],
            device_id={"grp": peer}, device_id_type=MESH,
        )

    int_copy = pltpu.make_async_copy(ints_hbm, ints, int_sem)
    int_copy.start()
    for i in range(chunks):
        key_copy(i).start()
    barrier = pltpu.get_barrier_semaphore()
    pl.semaphore_signal(barrier, inc=1, device_id={"grp": peer}, device_id_type=MESH)
    int_copy.wait()

    @pl.loop(0, width // chunk)
    def _(i):
        rows = pl.ds(pl.multiple_of(i * chunk, chunk), chunk)
        probes[rows, :] = (ints[rows, :].astype(jnp.float32) * 0.015625).astype(jnp.bfloat16)

    pl.semaphore_wait(barrier, 1)

    @pl.loop(0, chunks)
    def _(i):
        rows = pl.ds(pl.multiple_of(i * chunk, chunk), chunk)
        key_copy(i).wait()
        part[rows, :] = dot_f32(keys[rows, :], probes[...])
        swap(i).start()

    @pl.loop(0, chunks)
    def _(i):
        start = pl.multiple_of(i * chunk, chunk)
        rows = pl.ds(start, chunk)
        swap(i).wait()
        total = part[rows, :] + other[rows, :]
        sketch_ref[rows, :] = total
        flipped = total.T
        top = flipped.astype(jnp.bfloat16)
        high[:, rows] = top
        low[:, rows] = (flipped - top.astype(jnp.float32)).astype(jnp.bfloat16)

    for t, (row0, row1, col0, col1) in enumerate(
        ((0, 1, 0, 0), (3, 1, 0, 1), (3, 2, 1, 0), (3, 2, 2, 1), (3, 2, 3, 2))
    ):
        row = pl.multiple_of((row0 + group * (row1 - row0)) * BLOCK, BLOCK)
        col = pl.multiple_of((col0 + group * (col1 - col0)) * BLOCK, BLOCK)
        row_high, row_low = high[pl.ds(row, BLOCK), :], low[pl.ds(row, BLOCK), :]
        col_high, col_low = high[pl.ds(col, BLOCK), :], low[pl.ds(col, BLOCK), :]
        gram_ref[t] = dot_f32(row_high, col_high, LAST) + (
            dot_f32(row_high, col_low, LAST) + dot_f32(row_low, col_high, LAST)
        )

    @pl.loop(0, width // tile)
    def _(j):
        cols = pl.ds(pl.multiple_of(j * tile, tile), tile)
        product = dot_f32(high[...], keys[:, cols]) + dot_f32(low[...], keys[:, cols])
        basis_ref[cols, :] = product.T


def front(key_rows, probe_ints):
    tokens, width = key_rows.shape
    count = probe_ints.shape[1]
    chunk = 256
    chunks = tokens // chunk
    vmem = pl.BlockSpec(memory_space=pltpu.VMEM)
    anyspace = pl.BlockSpec(memory_space=pl.ANY)
    return pl.pallas_call(
        functools.partial(front_kernel, chunk, 256),
        out_shape=(
            jax.ShapeDtypeStruct((tokens, count), jnp.float32),
            jax.ShapeDtypeStruct((5, BLOCK, BLOCK), jnp.float32),
            jax.ShapeDtypeStruct((width, count), jnp.float32),
        ),
        in_specs=[anyspace, anyspace],
        out_specs=(vmem, vmem, vmem),
        scratch_shapes=[
            pltpu.VMEM((tokens, width), jnp.bfloat16),
            pltpu.VMEM((width, count), jnp.int32),
            pltpu.VMEM((width, count), jnp.bfloat16),
            pltpu.VMEM((tokens, count), jnp.float32),
            pltpu.VMEM((tokens, count), jnp.float32),
            pltpu.VMEM((count, tokens), jnp.bfloat16),
            pltpu.VMEM((count, tokens), jnp.bfloat16),
            pltpu.SemaphoreType.DMA((chunks,)),
            pltpu.SemaphoreType.DMA,
            pltpu.SemaphoreType.DMA((chunks,)),
            pltpu.SemaphoreType.DMA((chunks,)),
        ],
        compiler_params=pltpu.CompilerParams(
            collective_id=0, has_side_effects=True, vmem_limit_bytes=50 << 20
        ),
        name="front",
    )(key_rows, probe_ints)


def gram_kernel(n, x_ref, out_ref, inbox, send1, recv1, send2, recv2, send3, recv3):
    me = lax.axis_index("seq")
    group = lax.axis_index("grp")
    peer = 1 - group
    barrier = pltpu.get_barrier_semaphore()

    @pl.loop(1, n)
    def _(k):
        pl.semaphore_signal(
            barrier, inc=1, device_id={"seq": lax.rem(me + k, n)}, device_id_type=MESH
        )

    pl.semaphore_signal(barrier, inc=1, device_id={"grp": peer}, device_id_type=MESH)
    pl.semaphore_wait(barrier, n)

    def scatter(k):
        to = lax.rem(me + k, n)
        return pltpu.make_async_remote_copy(
            src_ref=x_ref.at[to], dst_ref=inbox.at[k],
            send_sem=send1.at[k], recv_sem=recv1.at[k],
            device_id={"seq": to}, device_id_type=MESH,
        )

    def gather(k):
        return pltpu.make_async_remote_copy(
            src_ref=out_ref.at[group, me], dst_ref=out_ref.at[group, me],
            send_sem=send2.at[k], recv_sem=recv2.at[k],
            device_id={"seq": lax.rem(me + k, n)}, device_id_type=MESH,
        )

    def hand_over(k):
        source = lax.rem(me + n - k, n)
        return pltpu.make_async_remote_copy(
            src_ref=out_ref.at[group, source], dst_ref=out_ref.at[group, source],
            send_sem=send3.at[k], recv_sem=recv3.at[k],
            device_id={"grp": peer}, device_id_type=MESH,
        )

    @pl.loop(1, n)
    def _(k):
        scatter(k).start()

    out_ref[group, me] = x_ref[me]

    @pl.loop(1, n)
    def _(k):
        scatter(k).wait_recv()
        out_ref[group, me] += inbox[k]

    @pl.loop(1, n)
    def _(k):
        gather(k).start()

    hand_over(0).start()

    @pl.loop(1, n)
    def _(k):
        gather(k).wait_recv()
        hand_over(k).start()

    @pl.loop(1, n)
    def _(k):
        scatter(k).wait_send()
        gather(k).wait_send()
        hand_over(k).wait()

    hand_over(0).wait()


def sum_gram(blocks, n):
    size = blocks.size // BLOCK
    part = size // n
    vmem = pl.BlockSpec(memory_space=pltpu.VMEM)
    whole = pl.pallas_call(
        functools.partial(gram_kernel, n),
        out_shape=jax.ShapeDtypeStruct((2, n, part, BLOCK), jnp.float32),
        in_specs=[vmem],
        out_specs=vmem,
        scratch_shapes=[pltpu.VMEM((n, part, BLOCK), jnp.float32)]
        + [pltpu.SemaphoreType.DMA((n,))] * 6,
        compiler_params=pltpu.CompilerParams(collective_id=1, has_side_effects=True),
        name="gram_sum",
    )(blocks.reshape(n, part, BLOCK))
    return whole.reshape(2, 5, BLOCK, BLOCK)


def factor_block(a):
    panels = a.shape[0] // 8
    shape = (8, a.shape[1])
    spread = lambda v: jnp.broadcast_to(v, shape)
    sub = lax.broadcasted_iota(jnp.int32, shape, 0)
    lane = lax.broadcasted_iota(jnp.int32, shape, 1)
    rows = [a[8 * p : 8 * p + 8, :] for p in range(panels)]
    unit = [jnp.where(lane == sub + 8 * p, 1.0, 0.0).astype(jnp.float32) for p in range(panels)]
    result = []
    for p in range(panels):
        left, right = rows[p], unit[p]
        column = [spread(left[:, 8 * p + m : 8 * p + m + 1]) for m in range(8)]
        inverse_pivot = jnp.zeros(shape, jnp.float32)
        pivots = jnp.ones(shape, jnp.float32)
        for j in range(8):
            pivot = spread(column[j][j : j + 1, :])
            reciprocal = 1.0 / pivot
            factor = jnp.where(sub > j, column[j] * reciprocal, 0.0)
            for m in range(j + 1, 8):
                column[m] = column[m] - factor * spread(column[m][j : j + 1, :])
            left = left - factor * spread(left[j : j + 1, :])
            right = right - factor * spread(right[j : j + 1, :])
            inverse_pivot = jnp.where(sub == j, reciprocal, inverse_pivot)
            pivots = jnp.where(sub == j, pivot, pivots)
        result.append(right * lax.rsqrt(pivots))
        if p == panels - 1:
            break
        left, right = left * inverse_pivot, right * inverse_pivot
        for j in range(7, 0, -1):
            factor = jnp.where(sub < j, column[j] * inverse_pivot, 0.0)
            left = left - factor * spread(left[j : j + 1, :])
            right = right - factor * spread(right[j : j + 1, :])
        lefts = [spread(left[j : j + 1, :]) for j in range(8)]
        rights = [spread(right[j : j + 1, :]) for j in range(8)]
        for i in range(p + 1, panels):
            row, other = rows[i], unit[i]
            for j in range(8):
                factor = spread(rows[i][:, 8 * p + j : 8 * p + j + 1])
                row = row - factor * lefts[j]
                other = other - factor * rights[j]
            rows[i], unit[i] = row, other
    return jnp.concatenate(result, axis=0)


def exact(a, b, dims=(((1,), (0,)), ((), ()))):
    return lax.dot_general(
        a, b, dims, precision=lax.Precision.HIGHEST, preferred_element_type=jnp.float32
    )


def inverse_kernel(gram_ref, out_ref, cols):
    size = out_ref.shape[0]
    blocks = size // BLOCK
    cols[...] = jnp.zeros_like(cols)
    places = (((0, 0), (3, 0), (3, 1), (3, 2), (3, 3)), ((1, 0), (1, 1), (2, 0), (2, 1), (2, 2)))
    for group in range(2):
        for t, (i, j) in enumerate(places[group]):
            cols[j, i * BLOCK : (i + 1) * BLOCK, :] = gram_ref[group, t]
    row = lax.broadcasted_iota(jnp.int32, (size, size), 0)
    col = lax.broadcasted_iota(jnp.int32, (size, size), 1)
    out_ref[...] = jnp.where(row == col, 1.0, 0.0).astype(jnp.float32)

    @pl.loop(0, blocks)
    def _(b):
        start = pl.multiple_of(b * BLOCK, BLOCK)
        own = pl.ds(start, BLOCK)
        small = factor_block(cols[b, own, :])
        done = exact(small, out_ref[own, :])
        out_ref[own, :] = done
        below = exact(cols[b], small, LAST)
        below = jnp.where(
            lax.broadcasted_iota(jnp.int32, (size, BLOCK), 0) >= start + BLOCK, below, 0.0
        )
        cols[b] = below
        out_ref[...] -= exact(below, done)
        for j in range(1, blocks):
            cols[j] = cols[j] - jnp.where(
                j > b, exact(below, cols[b, j * BLOCK : (j + 1) * BLOCK, :], LAST), 0.0
            )


def inverse_factor(gram, size):
    vmem = pl.BlockSpec(memory_space=pltpu.VMEM)
    return pl.pallas_call(
        inverse_kernel,
        out_shape=jax.ShapeDtypeStruct((size, size), jnp.float32),
        in_specs=[vmem],
        out_specs=vmem,
        scratch_shapes=[pltpu.VMEM((size // BLOCK, size, BLOCK), jnp.float32)],
        compiler_params=pltpu.CompilerParams(vmem_limit_bytes=24 << 20),
        cost_estimate=pl.CostEstimate(
            flops=40_000_000_000, bytes_accessed=3 << 20, transcendentals=0
        ),
        name="inverse_factor",
    )(gram)


def on_device(key_rows, probe_ints, rank_keep):
    seq_count = lax.axis_size("seq")
    tokens = key_rows.shape[0] * seq_count
    root_tokens = math.sqrt(tokens)
    sketch, gram_blocks, product = front(key_rows, probe_ints)
    mixed = lax.psum_scatter(product, "seq", scatter_dimension=0, tiled=True)
    gram = sum_gram(gram_blocks, seq_count)
    probe_count = sketch.shape[1]
    inverse = inverse_factor(gram, probe_count)
    part_width = probe_count // lax.axis_size("grp")
    first_column = lax.axis_index("grp") * part_width
    columns = first_column + jnp.arange(part_width)
    own_rows = lax.dynamic_slice_in_dim(inverse, first_column, part_width, 0)
    own_columns = lax.dot_general(sketch, own_rows, LAST, precision=lax.Precision.HIGH)
    latents = jnp.where(columns[None, :] < rank_keep[0], own_columns * root_tokens, jnp.float32(0.0))
    some_columns = lax.dot_general(inverse, mixed, LAST, precision=lax.Precision.HIGH)
    row_index = jnp.arange(probe_count)
    some_columns = jnp.where(row_index[:, None] < rank_keep[0], some_columns, jnp.float32(0.0))
    latent_basis = lax.all_to_all(some_columns, "seq", split_axis=0, concat_axis=1, tiled=True)
    return (latents, latent_basis)


def solution(mesh):
    in_specs = (P("seq", "grp"), P("grp", None), P())
    out_specs = (P("seq", "grp"), P("seq", "grp"))
    return jax.shard_map(
        on_device, mesh=mesh, in_specs=in_specs, out_specs=out_specs, check_vma=False
    )
```

```python
import functools
import math

import jax
import jax.numpy as jnp
from jax import lax
from jax.experimental import pallas as pl
from jax.experimental.pallas import tpu as pltpu
from jax.sharding import PartitionSpec as P

MESH = pl.DeviceIdType.MESH
BLOCK = 128
LAST = (((1,), (1,)), ((), ()))


def dot_f32(a, b, dims=(((1,), (0,)), ((), ()))):
    return lax.dot_general(a, b, dims, preferred_element_type=jnp.float32)


def front_kernel(
    chunk, tile, keys_hbm, ints_hbm, sketch_ref, gram_ref, basis_ref,
    keys, ints, probes, part, other, high, low, key_sem, int_sem, send_sem, recv_sem,
):
    tokens, width = keys.shape
    group = lax.axis_index("grp")
    peer = 1 - group
    chunks = tokens // chunk

    def key_copy(i):
        rows = pl.ds(pl.multiple_of(i * chunk, chunk), chunk)
        return pltpu.make_async_copy(keys_hbm.at[rows], keys.at[rows], key_sem.at[i])

    def swap(i):
        rows = pl.ds(pl.multiple_of(i * chunk, chunk), chunk)
        return pltpu.make_async_remote_copy(
            src_ref=part.at[rows], dst_ref=other.at[rows],
            send_sem=send_sem.at[i], recv_sem=recv_sem.at[i],
            device_id={"grp": peer}, device_id_type=MESH,
        )

    int_copy = pltpu.make_async_copy(ints_hbm, ints, int_sem)
    int_copy.start()
    for i in range(chunks):
        key_copy(i).start()
    barrier = pltpu.get_barrier_semaphore()
    pl.semaphore_signal(barrier, inc=1, device_id={"grp": peer}, device_id_type=MESH)
    int_copy.wait()

    @pl.loop(0, width // chunk)
    def _(i):
        rows = pl.ds(pl.multiple_of(i * chunk, chunk), chunk)
        probes[rows, :] = (ints[rows, :].astype(jnp.float32) * 0.015625).astype(jnp.bfloat16)

    pl.semaphore_wait(barrier, 1)

    @pl.loop(0, chunks)
    def _(i):
        rows = pl.ds(pl.multiple_of(i * chunk, chunk), chunk)
        key_copy(i).wait()
        part[rows, :] = dot_f32(keys[rows, :], probes[...])
        swap(i).start()

    @pl.loop(0, chunks)
    def _(i):
        start = pl.multiple_of(i * chunk, chunk)
        rows = pl.ds(start, chunk)
        swap(i).wait()
        total = part[rows, :] + other[rows, :]
        sketch_ref[rows, :] = total
        flipped = total.T
        top = flipped.astype(jnp.bfloat16)
        high[:, rows] = top
        low[:, rows] = (flipped - top.astype(jnp.float32)).astype(jnp.bfloat16)

    for t, (row0, row1, col0, col1) in enumerate(
        ((0, 1, 0, 0), (3, 1, 0, 1), (3, 2, 1, 0), (3, 2, 2, 1), (3, 2, 3, 2))
    ):
        row = pl.multiple_of((row0 + group * (row1 - row0)) * BLOCK, BLOCK)
        col = pl.multiple_of((col0 + group * (col1 - col0)) * BLOCK, BLOCK)
        row_high, row_low = high[pl.ds(row, BLOCK), :], low[pl.ds(row, BLOCK), :]
        col_high, col_low = high[pl.ds(col, BLOCK), :], low[pl.ds(col, BLOCK), :]
        gram_ref[t] = dot_f32(row_high, col_high, LAST) + (
            dot_f32(row_high, col_low, LAST) + dot_f32(row_low, col_high, LAST)
        )

    @pl.loop(0, width // tile)
    def _(j):
        cols = pl.ds(pl.multiple_of(j * tile, tile), tile)
        product = dot_f32(high[...], keys[:, cols]) + dot_f32(low[...], keys[:, cols])
        basis_ref[cols, :] = product.T


def front(key_rows, probe_ints):
    tokens, width = key_rows.shape
    count = probe_ints.shape[1]
    chunk = 256
    chunks = tokens // chunk
    vmem = pl.BlockSpec(memory_space=pltpu.VMEM)
    anyspace = pl.BlockSpec(memory_space=pl.ANY)
    return pl.pallas_call(
        functools.partial(front_kernel, chunk, 256),
        out_shape=(
            jax.ShapeDtypeStruct((tokens, count), jnp.float32),
            jax.ShapeDtypeStruct((5, BLOCK, BLOCK), jnp.float32),
            jax.ShapeDtypeStruct((width, count), jnp.float32),
        ),
        in_specs=[anyspace, anyspace],
        out_specs=(vmem, vmem, vmem),
        scratch_shapes=[
            pltpu.VMEM((tokens, width), jnp.bfloat16),
            pltpu.VMEM((width, count), jnp.int32),
            pltpu.VMEM((width, count), jnp.bfloat16),
            pltpu.VMEM((tokens, count), jnp.float32),
            pltpu.VMEM((tokens, count), jnp.float32),
            pltpu.VMEM((count, tokens), jnp.bfloat16),
            pltpu.VMEM((count, tokens), jnp.bfloat16),
            pltpu.SemaphoreType.DMA((chunks,)),
            pltpu.SemaphoreType.DMA,
            pltpu.SemaphoreType.DMA((chunks,)),
            pltpu.SemaphoreType.DMA((chunks,)),
        ],
        compiler_params=pltpu.CompilerParams(
            collective_id=0, has_side_effects=True, vmem_limit_bytes=50 << 20
        ),
        name="front",
    )(key_rows, probe_ints)


def factor_block(a):
    panels = a.shape[0] // 8
    shape = (8, a.shape[1])
    spread = lambda v: jnp.broadcast_to(v, shape)
    sub = lax.broadcasted_iota(jnp.int32, shape, 0)
    lane = lax.broadcasted_iota(jnp.int32, shape, 1)
    rows = [a[8 * p : 8 * p + 8, :] for p in range(panels)]
    unit = [jnp.where(lane == sub + 8 * p, 1.0, 0.0).astype(jnp.float32) for p in range(panels)]
    result = []
    for p in range(panels):
        left, right = rows[p], unit[p]
        column = [spread(left[:, 8 * p + m : 8 * p + m + 1]) for m in range(8)]
        inverse_pivot = jnp.zeros(shape, jnp.float32)
        pivots = jnp.ones(shape, jnp.float32)
        for j in range(8):
            pivot = spread(column[j][j : j + 1, :])
            reciprocal = 1.0 / pivot
            factor = jnp.where(sub > j, column[j] * reciprocal, 0.0)
            for m in range(j + 1, 8):
                column[m] = column[m] - factor * spread(column[m][j : j + 1, :])
            left = left - factor * spread(left[j : j + 1, :])
            right = right - factor * spread(right[j : j + 1, :])
            inverse_pivot = jnp.where(sub == j, reciprocal, inverse_pivot)
            pivots = jnp.where(sub == j, pivot, pivots)
        result.append(right * lax.rsqrt(pivots))
        if p == panels - 1:
            break
        left, right = left * inverse_pivot, right * inverse_pivot
        for j in range(7, 0, -1):
            factor = jnp.where(sub < j, column[j] * inverse_pivot, 0.0)
            left = left - factor * spread(left[j : j + 1, :])
            right = right - factor * spread(right[j : j + 1, :])
        lefts = [spread(left[j : j + 1, :]) for j in range(8)]
        rights = [spread(right[j : j + 1, :]) for j in range(8)]
        for i in range(p + 1, panels):
            row, other = rows[i], unit[i]
            for j in range(8):
                factor = spread(rows[i][:, 8 * p + j : 8 * p + j + 1])
                row = row - factor * lefts[j]
                other = other - factor * rights[j]
            rows[i], unit[i] = row, other
    return jnp.concatenate(result, axis=0)


def exact(a, b, dims=(((1,), (0,)), ((), ()))):
    return lax.dot_general(
        a, b, dims, precision=lax.Precision.HIGHEST, preferred_element_type=jnp.float32
    )


def middle_kernel(
    n, inner, x_ref, product, out_ref, mixed_ref, whole, inbox, cols, near, total, far,
    send1, recv1, send2, recv2, send3, recv3, near_send, near_recv, far_send, far_recv,
):
    me = lax.axis_index("seq")
    group = lax.axis_index("grp")
    peer = 1 - group
    outer = n // inner
    high, low = me // inner, lax.rem(me, inner)
    barrier = pltpu.get_barrier_semaphore()

    @pl.loop(1, n)
    def _(k):
        pl.semaphore_signal(
            barrier, inc=1, device_id={"seq": lax.rem(me + k, n)}, device_id_type=MESH
        )

    pl.semaphore_signal(barrier, inc=1, device_id={"grp": peer}, device_id_type=MESH)
    pl.semaphore_wait(barrier, n)

    def scatter(k):
        to = lax.rem(me + k, n)
        return pltpu.make_async_remote_copy(
            src_ref=x_ref.at[to], dst_ref=inbox.at[k],
            send_sem=send1.at[k], recv_sem=recv1.at[k],
            device_id={"seq": to}, device_id_type=MESH,
        )

    def gather(k):
        return pltpu.make_async_remote_copy(
            src_ref=whole.at[group, me], dst_ref=whole.at[group, me],
            send_sem=send2.at[k], recv_sem=recv2.at[k],
            device_id={"seq": lax.rem(me + k, n)}, device_id_type=MESH,
        )

    def hand_over(k):
        source = lax.rem(me + n - k, n)
        return pltpu.make_async_remote_copy(
            src_ref=whole.at[group, source], dst_ref=whole.at[group, source],
            send_sem=send3.at[k], recv_sem=recv3.at[k],
            device_id={"grp": peer}, device_id_type=MESH,
        )

    def send_near(k):
        to = lax.rem(low + k, inner)
        return pltpu.make_async_remote_copy(
            src_ref=product.at[:, to], dst_ref=near.at[k],
            send_sem=near_send.at[k], recv_sem=near_recv.at[k],
            device_id={"seq": high * inner + to}, device_id_type=MESH,
        )

    def send_far(k):
        to = lax.rem(high + k, outer)
        return pltpu.make_async_remote_copy(
            src_ref=total.at[to], dst_ref=far.at[k],
            send_sem=far_send.at[k], recv_sem=far_recv.at[k],
            device_id={"seq": to * inner + low}, device_id_type=MESH,
        )

    @pl.loop(1, n)
    def _(k):
        scatter(k).start()

    for k in range(1, inner):
        send_near(k).start()

    whole[group, me] = x_ref[me]

    @pl.loop(1, n)
    def _(k):
        scatter(k).wait_recv()
        whole[group, me] += inbox[k]

    @pl.loop(1, n)
    def _(k):
        gather(k).start()

    hand_over(0).start()

    @pl.loop(1, n)
    def _(k):
        gather(k).wait_recv()
        hand_over(k).start()

    @pl.loop(1, n)
    def _(k):
        scatter(k).wait_send()
        gather(k).wait_send()
        hand_over(k).wait()

    hand_over(0).wait()

    size = out_ref.shape[0]
    blocks = size // BLOCK
    part = x_ref.shape[1]
    cols[...] = jnp.zeros_like(cols)
    places = (((0, 0), (3, 0), (3, 1), (3, 2), (3, 3)), ((1, 0), (1, 1), (2, 0), (2, 1), (2, 2)))
    for side in range(2):
        flat = whole[side].reshape(n * part, BLOCK)
        for t, (i, j) in enumerate(places[side]):
            cols[j, i * BLOCK : (i + 1) * BLOCK, :] = flat[t * BLOCK : (t + 1) * BLOCK]
    row = lax.broadcasted_iota(jnp.int32, (size, size), 0)
    col = lax.broadcasted_iota(jnp.int32, (size, size), 1)
    out_ref[...] = jnp.where(row == col, 1.0, 0.0).astype(jnp.float32)

    @pl.loop(0, blocks)
    def _(b):
        @pl.when(b == blocks // 2)
        def _():
            for k in range(1, inner):
                send_near(k).wait()

            @pl.loop(0, outer)
            def _(h):
                value = product[h, low]
                for k in range(1, inner):
                    value = value + near[k, h]
                total[h] = value

            @pl.loop(1, outer)
            def _(k):
                send_far(k).start()

        start = pl.multiple_of(b * BLOCK, BLOCK)
        own = pl.ds(start, BLOCK)
        small = factor_block(cols[b, own, :])
        done = exact(small, out_ref[own, :])
        out_ref[own, :] = done
        below = exact(cols[b], small, LAST)
        below = jnp.where(
            lax.broadcasted_iota(jnp.int32, (size, BLOCK), 0) >= start + BLOCK, below, 0.0
        )
        cols[b] = below
        out_ref[...] -= exact(below, done)
        for j in range(1, blocks):
            cols[j] = cols[j] - jnp.where(
                j > b, exact(below, cols[b, j * BLOCK : (j + 1) * BLOCK, :], LAST), 0.0
            )

    mixed_ref[...] = total[high]

    @pl.loop(1, outer)
    def _(k):
        send_far(k).wait()
        mixed_ref[...] += far[k]


def middle(blocks, product, n):
    part = blocks.size // BLOCK // n
    width, size = product.shape
    rows = width // n
    inner = math.gcd(n, 4)
    outer = n // inner
    vmem = pl.BlockSpec(memory_space=pltpu.VMEM)
    sem = pltpu.SemaphoreType.DMA
    return pl.pallas_call(
        functools.partial(middle_kernel, n, inner),
        out_shape=(
            jax.ShapeDtypeStruct((size, size), jnp.float32),
            jax.ShapeDtypeStruct((rows, size), jnp.float32),
        ),
        in_specs=[vmem, vmem],
        out_specs=(vmem, vmem),
        scratch_shapes=[
            pltpu.VMEM((2, n, part, BLOCK), jnp.float32),
            pltpu.VMEM((n, part, BLOCK), jnp.float32),
            pltpu.VMEM((size // BLOCK, size, BLOCK), jnp.float32),
            pltpu.VMEM((inner, outer, rows, size), jnp.float32),
            pltpu.VMEM((outer, rows, size), jnp.float32),
            pltpu.VMEM((outer, rows, size), jnp.float32),
        ]
        + [sem((n,))] * 6
        + [sem((inner,))] * 2
        + [sem((outer,))] * 2,
        compiler_params=pltpu.CompilerParams(
            collective_id=1, has_side_effects=True, vmem_limit_bytes=40 << 20
        ),
        name="middle",
    )(blocks.reshape(n, part, BLOCK), product.reshape(outer, inner, rows, size))


def on_device(key_rows, probe_ints, rank_keep):
    seq_count = lax.axis_size("seq")
    tokens = key_rows.shape[0] * seq_count
    root_tokens = math.sqrt(tokens)
    sketch, gram_blocks, product = front(key_rows, probe_ints)
    inverse, mixed = middle(gram_blocks, product, seq_count)
    probe_count = sketch.shape[1]
    part_width = probe_count // lax.axis_size("grp")
    first_column = lax.axis_index("grp") * part_width
    columns = first_column + jnp.arange(part_width)
    own_rows = lax.dynamic_slice_in_dim(inverse, first_column, part_width, 0)
    own_columns = lax.dot_general(sketch, own_rows, LAST, precision=lax.Precision.HIGH)
    latents = jnp.where(columns[None, :] < rank_keep[0], own_columns * root_tokens, jnp.float32(0.0))
    some_columns = lax.dot_general(inverse, mixed, LAST, precision=lax.Precision.HIGH)
    row_index = jnp.arange(probe_count)
    some_columns = jnp.where(row_index[:, None] < rank_keep[0], some_columns, jnp.float32(0.0))
    latent_basis = lax.all_to_all(some_columns, "seq", split_axis=0, concat_axis=1, tiled=True)
    return (latents, latent_basis)


def solution(mesh):
    in_specs = (P("seq", "grp"), P("grp", None), P())
    out_specs = (P("seq", "grp"), P("seq", "grp"))
    return jax.shard_map(
        on_device, mesh=mesh, in_specs=in_specs, out_specs=out_specs, check_vma=False
    )
```

```python
import functools
import math

import jax
import jax.numpy as jnp
from jax import lax
from jax.experimental import pallas as pl
from jax.experimental.pallas import tpu as pltpu
from jax.sharding import PartitionSpec as P

MESH = pl.DeviceIdType.MESH
BLOCK = 128
LAST = (((1,), (1,)), ((), ()))


def dot_f32(a, b, dims=(((1,), (0,)), ((), ()))):
    return lax.dot_general(a, b, dims, preferred_element_type=jnp.float32)


def factor_block(a):
    panels = a.shape[0] // 8
    shape = (8, a.shape[1])
    spread = lambda v: jnp.broadcast_to(v, shape)
    sub = lax.broadcasted_iota(jnp.int32, shape, 0)
    lane = lax.broadcasted_iota(jnp.int32, shape, 1)
    rows = [a[8 * p : 8 * p + 8, :] for p in range(panels)]
    unit = [jnp.where(lane == sub + 8 * p, 1.0, 0.0).astype(jnp.float32) for p in range(panels)]
    result = []
    for p in range(panels):
        left, right = rows[p], unit[p]
        column = [spread(left[:, 8 * p + m : 8 * p + m + 1]) for m in range(8)]
        inverse_pivot = jnp.zeros(shape, jnp.float32)
        pivots = jnp.ones(shape, jnp.float32)
        for j in range(8):
            pivot = spread(column[j][j : j + 1, :])
            reciprocal = 1.0 / pivot
            factor = jnp.where(sub > j, column[j] * reciprocal, 0.0)
            for m in range(j + 1, 8):
                column[m] = column[m] - factor * spread(column[m][j : j + 1, :])
            left = left - factor * spread(left[j : j + 1, :])
            right = right - factor * spread(right[j : j + 1, :])
            inverse_pivot = jnp.where(sub == j, reciprocal, inverse_pivot)
            pivots = jnp.where(sub == j, pivot, pivots)
        result.append(right * lax.rsqrt(pivots))
        if p == panels - 1:
            break
        left, right = left * inverse_pivot, right * inverse_pivot
        for j in range(7, 0, -1):
            factor = jnp.where(sub < j, column[j] * inverse_pivot, 0.0)
            left = left - factor * spread(left[j : j + 1, :])
            right = right - factor * spread(right[j : j + 1, :])
        lefts = [spread(left[j : j + 1, :]) for j in range(8)]
        rights = [spread(right[j : j + 1, :]) for j in range(8)]
        for i in range(p + 1, panels):
            row, other = rows[i], unit[i]
            for j in range(8):
                factor = spread(rows[i][:, 8 * p + j : 8 * p + j + 1])
                row = row - factor * lefts[j]
                other = other - factor * rights[j]
            rows[i], unit[i] = row, other
    return jnp.concatenate(result, axis=0)


def exact(a, b, dims=(((1,), (0,)), ((), ()))):
    return lax.dot_general(
        a, b, dims, precision=lax.Precision.HIGHEST, preferred_element_type=jnp.float32
    )


def whole_kernel(
    n, inner, chunk, tile, keys_hbm, ints_hbm, sketch_hbm, out_ref, mixed_ref,
    keys, ints, probes, part, other, high, low, packed, product,
    whole, inbox, cols, near, total, far,
    key_sem, int_sem, sketch_sem, send_sem, recv_sem,
    send1, recv1, send2, recv2, send3, recv3, near_send, near_recv, far_send, far_recv,
):
    tokens, width = keys.shape
    me = lax.axis_index("seq")
    group = lax.axis_index("grp")
    peer = 1 - group
    outer = n // inner
    mine, place = me // inner, lax.rem(me, inner)
    chunks = tokens // chunk
    size = out_ref.shape[0]
    blocks = size // BLOCK
    rows_each = product.shape[2]
    step = rows_each // blocks

    def key_copy(i):
        rows = pl.ds(pl.multiple_of(i * chunk, chunk), chunk)
        return pltpu.make_async_copy(keys_hbm.at[rows], keys.at[rows], key_sem.at[i])

    def swap(i):
        rows = pl.ds(pl.multiple_of(i * chunk, chunk), chunk)
        return pltpu.make_async_remote_copy(
            src_ref=part.at[rows], dst_ref=other.at[rows],
            send_sem=send_sem.at[i], recv_sem=recv_sem.at[i],
            device_id={"grp": peer}, device_id_type=MESH,
        )

    int_copy = pltpu.make_async_copy(ints_hbm, ints, int_sem)
    int_copy.start()
    for i in range(chunks):
        key_copy(i).start()
    barrier = pltpu.get_barrier_semaphore()

    @pl.loop(1, n)
    def _(k):
        pl.semaphore_signal(
            barrier, inc=1, device_id={"seq": lax.rem(me + k, n)}, device_id_type=MESH
        )

    pl.semaphore_signal(barrier, inc=1, device_id={"grp": peer}, device_id_type=MESH)
    int_copy.wait()

    @pl.loop(0, width // chunk)
    def _(i):
        rows = pl.ds(pl.multiple_of(i * chunk, chunk), chunk)
        probes[rows, :] = (ints[rows, :].astype(jnp.float32) * 0.015625).astype(jnp.bfloat16)

    pl.semaphore_wait(barrier, n)

    @pl.loop(0, chunks)
    def _(i):
        rows = pl.ds(pl.multiple_of(i * chunk, chunk), chunk)
        key_copy(i).wait()
        part[rows, :] = dot_f32(keys[rows, :], probes[...])
        swap(i).start()

    @pl.loop(0, chunks)
    def _(i):
        start = pl.multiple_of(i * chunk, chunk)
        rows = pl.ds(start, chunk)
        swap(i).wait()
        summed = part[rows, :] + other[rows, :]
        part[rows, :] = summed
        flipped = summed.T
        top = flipped.astype(jnp.bfloat16)
        high[:, rows] = top
        low[:, rows] = (flipped - top.astype(jnp.float32)).astype(jnp.bfloat16)

    def scatter(k):
        to = lax.rem(me + k, n)
        return pltpu.make_async_remote_copy(
            src_ref=packed.at[to], dst_ref=inbox.at[k],
            send_sem=send1.at[k], recv_sem=recv1.at[k],
            device_id={"seq": to}, device_id_type=MESH,
        )

    def gather(k):
        return pltpu.make_async_remote_copy(
            src_ref=whole.at[group, me], dst_ref=whole.at[group, me],
            send_sem=send2.at[k], recv_sem=recv2.at[k],
            device_id={"seq": lax.rem(me + k, n)}, device_id_type=MESH,
        )

    def hand_over(k):
        source = lax.rem(me + n - k, n)
        return pltpu.make_async_remote_copy(
            src_ref=whole.at[group, source], dst_ref=whole.at[group, source],
            send_sem=send3.at[k], recv_sem=recv3.at[k],
            device_id={"grp": peer}, device_id_type=MESH,
        )

    def piece(c):
        return pl.ds(pl.multiple_of(c * step, step), step)

    def send_near(c, k):
        to = lax.rem(place + k, inner)
        return pltpu.make_async_remote_copy(
            src_ref=product.at[:, to, piece(c)], dst_ref=near.at[k, :, piece(c)],
            send_sem=near_send.at[c, k], recv_sem=near_recv.at[c, k],
            device_id={"seq": mine * inner + to}, device_id_type=MESH,
        )

    def send_far(c, k):
        to = lax.rem(mine + k, outer)
        return pltpu.make_async_remote_copy(
            src_ref=total.at[to, piece(c)], dst_ref=far.at[k, piece(c)],
            send_sem=far_send.at[c, k], recv_sem=far_recv.at[c, k],
            device_id={"seq": to * inner + place}, device_id_type=MESH,
        )

    def pass_on(c):
        for k in range(1, inner):
            send_near(c, k).wait()

        @pl.loop(0, outer)
        def _(h):
            value = product[h, place, piece(c), :]
            for k in range(1, inner):
                value = value + near[k, h, piece(c), :]
            total[h, piece(c), :] = value

        @pl.loop(1, outer)
        def _(k):
            send_far(c, k).start()

    sketch_copy = pltpu.make_async_copy(part, sketch_hbm, sketch_sem)
    sketch_copy.start()

    found = []
    for t, (row0, row1, col0, col1) in enumerate(
        ((0, 1, 0, 0), (3, 1, 0, 1), (3, 2, 1, 0), (3, 2, 2, 1), (3, 2, 3, 2))
    ):
        row = pl.multiple_of((row0 + group * (row1 - row0)) * BLOCK, BLOCK)
        col = pl.multiple_of((col0 + group * (col1 - col0)) * BLOCK, BLOCK)
        row_high, row_low = high[pl.ds(row, BLOCK), :], low[pl.ds(row, BLOCK), :]
        col_high, col_low = high[pl.ds(col, BLOCK), :], low[pl.ds(col, BLOCK), :]
        found.append(
            dot_f32(row_high, col_high, LAST)
            + (dot_f32(row_high, col_low, LAST) + dot_f32(row_low, col_high, LAST))
        )

    packed[...] = jnp.concatenate(found, axis=0).reshape(packed.shape)

    @pl.loop(1, n)
    def _(k):
        scatter(k).start()

    @pl.loop(0, width // tile)
    def _(j):
        own = pl.ds(pl.multiple_of(j * tile, tile), tile)
        piled = (dot_f32(high[...], keys[:, own]) + dot_f32(low[...], keys[:, own])).T
        for u in range(tile // rows_each):
            q = j * (tile // rows_each) + u
            product[q // inner, lax.rem(q, inner)] = piled[u * rows_each : (u + 1) * rows_each]

    whole[group, me] = packed[me]

    @pl.loop(1, n)
    def _(k):
        scatter(k).wait_recv()
        whole[group, me] += inbox[k]

    @pl.loop(1, n)
    def _(k):
        gather(k).start()

    hand_over(0).start()

    for k in range(1, inner):
        send_near(0, k).start()

    @pl.loop(1, n)
    def _(k):
        gather(k).wait_recv()
        hand_over(k).start()

    for c in range(1, blocks):
        for k in range(1, inner):
            send_near(c, k).start()

    @pl.loop(1, n)
    def _(k):
        scatter(k).wait_send()
        gather(k).wait_send()
        hand_over(k).wait()

    hand_over(0).wait()

    cols[...] = jnp.zeros_like(cols)
    places = (((0, 0), (3, 0), (3, 1), (3, 2), (3, 3)), ((1, 0), (1, 1), (2, 0), (2, 1), (2, 2)))
    for side in range(2):
        flat = whole[side].reshape(n * packed.shape[1], BLOCK)
        for t, (i, j) in enumerate(places[side]):
            cols[j, i * BLOCK : (i + 1) * BLOCK, :] = flat[t * BLOCK : (t + 1) * BLOCK]
    row = lax.broadcasted_iota(jnp.int32, (size, size), 0)
    col = lax.broadcasted_iota(jnp.int32, (size, size), 1)
    out_ref[...] = jnp.where(row == col, 1.0, 0.0).astype(jnp.float32)

    @pl.loop(0, blocks)
    def _(b):
        @pl.when(b >= 1)
        def _():
            pass_on(b - 1)

        start = pl.multiple_of(b * BLOCK, BLOCK)
        own = pl.ds(start, BLOCK)
        small = factor_block(cols[b, own, :])
        done = exact(small, out_ref[own, :])
        out_ref[own, :] = done
        below = exact(cols[b], small, LAST)
        below = jnp.where(
            lax.broadcasted_iota(jnp.int32, (size, BLOCK), 0) >= start + BLOCK, below, 0.0
        )
        cols[b] = below
        out_ref[...] -= exact(below, done)
        for j in range(1, blocks):
            cols[j] = cols[j] - jnp.where(
                j > b, exact(below, cols[b, j * BLOCK : (j + 1) * BLOCK, :], LAST), 0.0
            )

    pass_on(blocks - 1)
    sketch_copy.wait()
    mixed_ref[...] = total[mine]

    @pl.loop(0, blocks)
    def _(c):
        @pl.loop(1, outer)
        def _(k):
            send_far(c, k).wait()
            mixed_ref[piece(c), :] += far[k, piece(c), :]


def run_whole(key_rows, probe_ints, n):
    tokens, width = key_rows.shape
    size = probe_ints.shape[1]
    chunk, tile = 256, 256
    chunks, blocks = tokens // chunk, size // BLOCK
    part = 5 * BLOCK // n
    rows = width // n
    inner = math.gcd(n, 4)
    outer = n // inner
    vmem = pl.BlockSpec(memory_space=pltpu.VMEM)
    anyspace = pl.BlockSpec(memory_space=pl.ANY)
    sem = pltpu.SemaphoreType.DMA
    return pl.pallas_call(
        functools.partial(whole_kernel, n, inner, chunk, tile),
        out_shape=(
            jax.ShapeDtypeStruct((tokens, size), jnp.float32),
            jax.ShapeDtypeStruct((size, size), jnp.float32),
            jax.ShapeDtypeStruct((rows, size), jnp.float32),
        ),
        in_specs=[anyspace, anyspace],
        out_specs=(anyspace, vmem, vmem),
        scratch_shapes=[
            pltpu.VMEM((tokens, width), jnp.bfloat16),
            pltpu.VMEM((width, size), jnp.int32),
            pltpu.VMEM((width, size), jnp.bfloat16),
            pltpu.VMEM((tokens, size), jnp.float32),
            pltpu.VMEM((tokens, size), jnp.float32),
            pltpu.VMEM((size, tokens), jnp.bfloat16),
            pltpu.VMEM((size, tokens), jnp.bfloat16),
            pltpu.VMEM((n, part, BLOCK), jnp.float32),
            pltpu.VMEM((outer, inner, rows, size), jnp.float32),
            pltpu.VMEM((2, n, part, BLOCK), jnp.float32),
            pltpu.VMEM((n, part, BLOCK), jnp.float32),
            pltpu.VMEM((blocks, size, BLOCK), jnp.float32),
            pltpu.VMEM((inner, outer, rows, size), jnp.float32),
            pltpu.VMEM((outer, rows, size), jnp.float32),
            pltpu.VMEM((outer, rows, size), jnp.float32),
            sem((chunks,)), sem, sem, sem((chunks,)), sem((chunks,)),
        ]
        + [sem((n,))] * 6
        + [sem((blocks, inner))] * 2
        + [sem((blocks, outer))] * 2,
        compiler_params=pltpu.CompilerParams(
            collective_id=0, has_side_effects=True, vmem_limit_bytes=56 << 20
        ),
        name="whole",
    )(key_rows, probe_ints)


def on_device(key_rows, probe_ints, rank_keep):
    seq_count = lax.axis_size("seq")
    tokens = key_rows.shape[0] * seq_count
    root_tokens = math.sqrt(tokens)
    sketch, inverse, mixed = run_whole(key_rows, probe_ints, seq_count)
    probe_count = sketch.shape[1]
    part_width = probe_count // lax.axis_size("grp")
    first_column = lax.axis_index("grp") * part_width
    columns = first_column + jnp.arange(part_width)
    own_rows = lax.dynamic_slice_in_dim(inverse, first_column, part_width, 0)
    own_columns = lax.dot_general(sketch, own_rows, LAST, precision=lax.Precision.HIGH)
    latents = jnp.where(columns[None, :] < rank_keep[0], own_columns * root_tokens, jnp.float32(0.0))
    some_columns = lax.dot_general(inverse, mixed, LAST, precision=lax.Precision.HIGH)
    row_index = jnp.arange(probe_count)
    some_columns = jnp.where(row_index[:, None] < rank_keep[0], some_columns, jnp.float32(0.0))
    latent_basis = lax.all_to_all(some_columns, "seq", split_axis=0, concat_axis=1, tiled=True)
    return (latents, latent_basis)


def solution(mesh):
    in_specs = (P("seq", "grp"), P("grp", None), P())
    out_specs = (P("seq", "grp"), P("seq", "grp"))
    return jax.shard_map(
        on_device, mesh=mesh, in_specs=in_specs, out_specs=out_specs, check_vma=False
    )
```

```python
import functools
import math

import jax
import jax.numpy as jnp
from jax import lax
from jax.experimental import pallas as pl
from jax.experimental.pallas import tpu as pltpu
from jax.sharding import PartitionSpec as P

MESH = pl.DeviceIdType.MESH
BLOCK = 128
LAST = (((1,), (1,)), ((), ()))


def dot_f32(a, b, dims=(((1,), (0,)), ((), ()))):
    return lax.dot_general(a, b, dims, preferred_element_type=jnp.float32)


def factor_block(a):
    panels = a.shape[0] // 8
    shape = (8, a.shape[1])
    spread = lambda v: jnp.broadcast_to(v, shape)
    sub = lax.broadcasted_iota(jnp.int32, shape, 0)
    lane = lax.broadcasted_iota(jnp.int32, shape, 1)
    rows = [a[8 * p : 8 * p + 8, :] for p in range(panels)]
    unit = [jnp.where(lane == sub + 8 * p, 1.0, 0.0).astype(jnp.float32) for p in range(panels)]
    result = []
    for p in range(panels):
        left, right = rows[p], unit[p]
        column = [spread(left[:, 8 * p + m : 8 * p + m + 1]) for m in range(8)]
        inverse_pivot = jnp.zeros(shape, jnp.float32)
        pivots = jnp.ones(shape, jnp.float32)
        for j in range(8):
            pivot = spread(column[j][j : j + 1, :])
            reciprocal = 1.0 / pivot
            factor = jnp.where(sub > j, column[j] * reciprocal, 0.0)
            for m in range(j + 1, 8):
                column[m] = column[m] - factor * spread(column[m][j : j + 1, :])
            left = left - factor * spread(left[j : j + 1, :])
            right = right - factor * spread(right[j : j + 1, :])
            inverse_pivot = jnp.where(sub == j, reciprocal, inverse_pivot)
            pivots = jnp.where(sub == j, pivot, pivots)
        result.append(right * lax.rsqrt(pivots))
        if p == panels - 1:
            break
        left, right = left * inverse_pivot, right * inverse_pivot
        for j in range(7, 0, -1):
            factor = jnp.where(sub < j, column[j] * inverse_pivot, 0.0)
            left = left - factor * spread(left[j : j + 1, :])
            right = right - factor * spread(right[j : j + 1, :])
        lefts = [spread(left[j : j + 1, :]) for j in range(8)]
        rights = [spread(right[j : j + 1, :]) for j in range(8)]
        for i in range(p + 1, panels):
            row, other = rows[i], unit[i]
            for j in range(8):
                factor = spread(rows[i][:, 8 * p + j : 8 * p + j + 1])
                row = row - factor * lefts[j]
                other = other - factor * rights[j]
            rows[i], unit[i] = row, other
    return jnp.concatenate(result, axis=0)


def exact(a, b, dims=(((1,), (0,)), ((), ()))):
    return lax.dot_general(
        a, b, dims, precision=lax.Precision.HIGHEST, preferred_element_type=jnp.float32
    )


def whole_kernel(
    n, inner, chunk, tile, root_tokens, keys_hbm, ints_hbm, latent_ref, spread_ref,
    out_ref, mixed_ref, boxed, arrived,
    keys, ints, probes, part, other, high, low, packed, product,
    whole, inbox, cols, near, total, far,
    key_sem, int_sem, send_sem, recv_sem, send4, recv4,
    send1, recv1, send2, recv2, send3, recv3, near_send, near_recv, far_send, far_recv,
):
    tokens, width = keys.shape
    me = lax.axis_index("seq")
    group = lax.axis_index("grp")
    peer = 1 - group
    outer = n // inner
    mine, place = me // inner, lax.rem(me, inner)
    chunks = tokens // chunk
    size = out_ref.shape[0]
    blocks = size // BLOCK
    rows_each = product.shape[2]
    step = rows_each // blocks

    def key_copy(i):
        rows = pl.ds(pl.multiple_of(i * chunk, chunk), chunk)
        return pltpu.make_async_copy(keys_hbm.at[rows], keys.at[rows], key_sem.at[i])

    def swap(i):
        rows = pl.ds(pl.multiple_of(i * chunk, chunk), chunk)
        return pltpu.make_async_remote_copy(
            src_ref=part.at[rows], dst_ref=other.at[rows],
            send_sem=send_sem.at[i], recv_sem=recv_sem.at[i],
            device_id={"grp": peer}, device_id_type=MESH,
        )

    int_copy = pltpu.make_async_copy(ints_hbm, ints, int_sem)
    int_copy.start()
    for i in range(chunks):
        key_copy(i).start()
    barrier = pltpu.get_barrier_semaphore()

    @pl.loop(1, n)
    def _(k):
        pl.semaphore_signal(
            barrier, inc=1, device_id={"seq": lax.rem(me + k, n)}, device_id_type=MESH
        )

    pl.semaphore_signal(barrier, inc=1, device_id={"grp": peer}, device_id_type=MESH)
    int_copy.wait()

    @pl.loop(0, width // chunk)
    def _(i):
        rows = pl.ds(pl.multiple_of(i * chunk, chunk), chunk)
        probes[rows, :] = (ints[rows, :].astype(jnp.float32) * 0.015625).astype(jnp.bfloat16)

    pl.semaphore_wait(barrier, n)

    @pl.loop(0, chunks)
    def _(i):
        rows = pl.ds(pl.multiple_of(i * chunk, chunk), chunk)
        key_copy(i).wait()
        part[rows, :] = dot_f32(keys[rows, :], probes[...])
        swap(i).start()

    @pl.loop(0, chunks)
    def _(i):
        start = pl.multiple_of(i * chunk, chunk)
        rows = pl.ds(start, chunk)
        swap(i).wait()
        summed = part[rows, :] + other[rows, :]
        part[rows, :] = summed
        flipped = summed.T
        top = flipped.astype(jnp.bfloat16)
        high[:, rows] = top
        low[:, rows] = (flipped - top.astype(jnp.float32)).astype(jnp.bfloat16)

    def scatter(k):
        to = lax.rem(me + k, n)
        return pltpu.make_async_remote_copy(
            src_ref=packed.at[to], dst_ref=inbox.at[k],
            send_sem=send1.at[k], recv_sem=recv1.at[k],
            device_id={"seq": to}, device_id_type=MESH,
        )

    def gather(k):
        return pltpu.make_async_remote_copy(
            src_ref=whole.at[group, me], dst_ref=whole.at[group, me],
            send_sem=send2.at[k], recv_sem=recv2.at[k],
            device_id={"seq": lax.rem(me + k, n)}, device_id_type=MESH,
        )

    def hand_over(k):
        source = lax.rem(me + n - k, n)
        return pltpu.make_async_remote_copy(
            src_ref=whole.at[group, source], dst_ref=whole.at[group, source],
            send_sem=send3.at[k], recv_sem=recv3.at[k],
            device_id={"grp": peer}, device_id_type=MESH,
        )

    def piece(c):
        return pl.ds(pl.multiple_of(c * step, step), step)

    def send_near(c, k):
        to = lax.rem(place + k, inner)
        return pltpu.make_async_remote_copy(
            src_ref=product.at[:, to, piece(c)], dst_ref=near.at[k, :, piece(c)],
            send_sem=near_send.at[c, k], recv_sem=near_recv.at[c, k],
            device_id={"seq": mine * inner + to}, device_id_type=MESH,
        )

    def send_far(c, k):
        to = lax.rem(mine + k, outer)
        return pltpu.make_async_remote_copy(
            src_ref=total.at[to, piece(c)], dst_ref=far.at[k, piece(c)],
            send_sem=far_send.at[c, k], recv_sem=far_recv.at[c, k],
            device_id={"seq": to * inner + place}, device_id_type=MESH,
        )

    def pass_on(c):
        for k in range(1, inner):
            send_near(c, k).wait()

        @pl.loop(0, outer)
        def _(h):
            value = product[h, place, piece(c), :]
            for k in range(1, inner):
                value = value + near[k, h, piece(c), :]
            total[h, piece(c), :] = value

        @pl.loop(1, outer)
        def _(k):
            send_far(c, k).start()

    found = []
    for t, (row0, row1, col0, col1) in enumerate(
        ((0, 1, 0, 0), (3, 1, 0, 1), (3, 2, 1, 0), (3, 2, 2, 1), (3, 2, 3, 2))
    ):
        row = pl.multiple_of((row0 + group * (row1 - row0)) * BLOCK, BLOCK)
        col = pl.multiple_of((col0 + group * (col1 - col0)) * BLOCK, BLOCK)
        row_high, row_low = high[pl.ds(row, BLOCK), :], low[pl.ds(row, BLOCK), :]
        col_high, col_low = high[pl.ds(col, BLOCK), :], low[pl.ds(col, BLOCK), :]
        found.append(
            dot_f32(row_high, col_high, LAST)
            + (dot_f32(row_high, col_low, LAST) + dot_f32(row_low, col_high, LAST))
        )

    packed[...] = jnp.concatenate(found, axis=0).reshape(packed.shape)

    @pl.loop(1, n)
    def _(k):
        scatter(k).start()

    @pl.loop(0, width // tile)
    def _(j):
        own = pl.ds(pl.multiple_of(j * tile, tile), tile)
        piled = (dot_f32(high[...], keys[:, own]) + dot_f32(low[...], keys[:, own])).T
        for u in range(tile // rows_each):
            q = j * (tile // rows_each) + u
            product[q // inner, lax.rem(q, inner)] = piled[u * rows_each : (u + 1) * rows_each]

    whole[group, me] = packed[me]

    @pl.loop(1, n)
    def _(k):
        scatter(k).wait_recv()
        whole[group, me] += inbox[k]

    @pl.loop(1, n)
    def _(k):
        gather(k).start()

    hand_over(0).start()

    for k in range(1, inner):
        send_near(0, k).start()

    @pl.loop(1, n)
    def _(k):
        gather(k).wait_recv()
        hand_over(k).start()

    for c in range(1, blocks):
        for k in range(1, inner):
            send_near(c, k).start()

    @pl.loop(1, n)
    def _(k):
        scatter(k).wait_send()
        gather(k).wait_send()
        hand_over(k).wait()

    hand_over(0).wait()

    cols[...] = jnp.zeros_like(cols)
    places = (((0, 0), (3, 0), (3, 1), (3, 2), (3, 3)), ((1, 0), (1, 1), (2, 0), (2, 1), (2, 2)))
    for side in range(2):
        flat = whole[side].reshape(n * packed.shape[1], BLOCK)
        for t, (i, j) in enumerate(places[side]):
            cols[j, i * BLOCK : (i + 1) * BLOCK, :] = flat[t * BLOCK : (t + 1) * BLOCK]
    row = lax.broadcasted_iota(jnp.int32, (size, size), 0)
    col = lax.broadcasted_iota(jnp.int32, (size, size), 1)
    out_ref[...] = jnp.where(row == col, 1.0, 0.0).astype(jnp.float32)

    @pl.loop(0, blocks)
    def _(b):
        @pl.when(b >= 1)
        def _():
            pass_on(b - 1)

        start = pl.multiple_of(b * BLOCK, BLOCK)
        own = pl.ds(start, BLOCK)
        small = factor_block(cols[b, own, :])
        done = exact(small, out_ref[own, :])
        out_ref[own, :] = done
        below = exact(cols[b], small, LAST)
        below = jnp.where(
            lax.broadcasted_iota(jnp.int32, (size, BLOCK), 0) >= start + BLOCK, below, 0.0
        )
        cols[b] = below
        out_ref[...] -= exact(below, done)
        for j in range(1, blocks):
            cols[j] = cols[j] - jnp.where(
                j > b, exact(below, cols[b, j * BLOCK : (j + 1) * BLOCK, :], LAST), 0.0
            )

    pass_on(blocks - 1)
    span = latent_ref.shape[1]
    inverse = out_ref[pl.ds(pl.multiple_of(group * span, span), span), :]
    inverse_high = inverse.astype(jnp.bfloat16)
    inverse_low = (inverse - inverse_high.astype(jnp.float32)).astype(jnp.bfloat16)

    def latents(first, last):
        @pl.loop(first, last)
        def _(i):
            rows = pl.ds(pl.multiple_of(i * chunk, chunk), chunk)
            value = part[rows, :]
            top = value.astype(jnp.bfloat16)
            rest = (value - top.astype(jnp.float32)).astype(jnp.bfloat16)
            latent_ref[rows, :] = root_tokens * (
                dot_f32(top, inverse_high, LAST)
                + (dot_f32(top, inverse_low, LAST) + dot_f32(rest, inverse_high, LAST))
            )

    def deal(k):
        to = lax.rem(me + k, n)
        return pltpu.make_async_remote_copy(
            src_ref=boxed.at[to], dst_ref=arrived.at[me],
            send_sem=send4.at[k], recv_sem=recv4.at[k],
            device_id={"seq": to}, device_id_type=MESH,
        )

    latents(0, chunks // 2)
    mixed_ref[...] = total[mine]

    @pl.loop(0, blocks)
    def _(c):
        @pl.loop(1, outer)
        def _(k):
            send_far(c, k).wait()
            mixed_ref[piece(c), :] += far[k, piece(c), :]

    boxed[...] = exact(out_ref[...], mixed_ref[...], LAST).reshape(boxed.shape)

    @pl.loop(1, n)
    def _(k):
        deal(k).start()

    arrived[me] = boxed[me]
    latents(chunks // 2, chunks)

    @pl.loop(1, n)
    def _(k):
        deal(k).wait()

    spread_ref[...] = arrived[...]


def run_whole(key_rows, probe_ints, n, span, root_tokens):
    tokens, width = key_rows.shape
    size = probe_ints.shape[1]
    chunk, tile = 256, 256
    chunks, blocks = tokens // chunk, size // BLOCK
    part = 5 * BLOCK // n
    rows = width // n
    inner = math.gcd(n, 4)
    outer = n // inner
    vmem = pl.BlockSpec(memory_space=pltpu.VMEM)
    anyspace = pl.BlockSpec(memory_space=pl.ANY)
    sem = pltpu.SemaphoreType.DMA
    return pl.pallas_call(
        functools.partial(whole_kernel, n, inner, chunk, tile, root_tokens),
        out_shape=(
            jax.ShapeDtypeStruct((tokens, span), jnp.float32),
            jax.ShapeDtypeStruct((n, size // n, rows), jnp.float32),
        ),
        in_specs=[anyspace, anyspace],
        out_specs=(vmem, vmem),
        scratch_shapes=[
            pltpu.VMEM((size, size), jnp.float32),
            pltpu.VMEM((rows, size), jnp.float32),
            pltpu.VMEM((n, size // n, rows), jnp.float32),
            pltpu.VMEM((n, size // n, rows), jnp.float32),
            pltpu.VMEM((tokens, width), jnp.bfloat16),
            pltpu.VMEM((width, size), jnp.int32),
            pltpu.VMEM((width, size), jnp.bfloat16),
            pltpu.VMEM((tokens, size), jnp.float32),
            pltpu.VMEM((tokens, size), jnp.float32),
            pltpu.VMEM((size, tokens), jnp.bfloat16),
            pltpu.VMEM((size, tokens), jnp.bfloat16),
            pltpu.VMEM((n, part, BLOCK), jnp.float32),
            pltpu.VMEM((outer, inner, rows, size), jnp.float32),
            pltpu.VMEM((2, n, part, BLOCK), jnp.float32),
            pltpu.VMEM((n, part, BLOCK), jnp.float32),
            pltpu.VMEM((blocks, size, BLOCK), jnp.float32),
            pltpu.VMEM((inner, outer, rows, size), jnp.float32),
            pltpu.VMEM((outer, rows, size), jnp.float32),
            pltpu.VMEM((outer, rows, size), jnp.float32),
            sem((chunks,)), sem, sem((chunks,)), sem((chunks,)),
        ]
        + [sem((n,))] * 8
        + [sem((blocks, inner))] * 2
        + [sem((blocks, outer))] * 2,
        compiler_params=pltpu.CompilerParams(
            collective_id=0, has_side_effects=True, vmem_limit_bytes=56 << 20
        ),
        name="whole",
    )(key_rows, probe_ints)


def on_device(key_rows, probe_ints, rank_keep):
    seq_count = lax.axis_size("seq")
    tokens = key_rows.shape[0] * seq_count
    root_tokens = math.sqrt(tokens)
    probe_count = probe_ints.shape[1]
    part_width = probe_count // lax.axis_size("grp")
    own_columns, dealt = run_whole(key_rows, probe_ints, seq_count, part_width, root_tokens)
    columns = lax.axis_index("grp") * part_width + jnp.arange(part_width)
    latents = jnp.where(columns[None, :] < rank_keep[0], own_columns, jnp.float32(0.0))
    rows_out = probe_count // seq_count
    row_index = lax.axis_index("seq") * rows_out + jnp.arange(rows_out)
    own_rows = jnp.transpose(dealt, (1, 0, 2)).reshape(rows_out, -1)
    latent_basis = jnp.where(row_index[:, None] < rank_keep[0], own_rows, jnp.float32(0.0))
    return (latents, latent_basis)


def solution(mesh):
    in_specs = (P("seq", "grp"), P("grp", None), P())
    out_specs = (P("seq", "grp"), P("seq", "grp"))
    return jax.shard_map(
        on_device, mesh=mesh, in_specs=in_specs, out_specs=out_specs, check_vma=False
    )
```
